256 devices in a mesh: row: 8 (over x, y_hi), col: 32 (over y_lo, z, core).
Axes of the slice: x: 4, y: 4 (y_hi: 2, y_lo: 2; y = y_hi * 2 + y_lo), z: 8, core: 2. Of those that a mesh axis runs over, the one named last changes fastest.
Arguments:
- ba_left: bfloat16 [32, 2048, 128], P('col', 'row'), may hold values from -6 to 6
- ba_right: bfloat16 [32, 2048, 128], P('col', 'row'), may hold values from -0.046875 to 0.046875
- l_inverse: bfloat16 [2048, 2048], P('row', 'col'), may hold values from -1 to 1, as said below
- aa_left: bfloat16 [32, 32, 2048, 128], P('row', 'col'), may hold values from -6 to 6
- aa_right: bfloat16 [32, 32, 2048, 128], P('row', 'col'), may hold values from -0.5 to 0.5
- sketch: bfloat16 [2048, 128], replicated, may hold values from -6 to 6
- cross_tile_ranks: int32 [32], P('col'), may hold values from 32 to 128
- aa_rank: int32 [32, 32], P('row', 'col'), may hold values from 96 to 128
- target_rank: int32 [32, 32], P('row', 'col'), may hold values from 16 to 64
Outputs:
- new_left: bfloat16 [32, 32, 2048, 128], P('row', 'col')
- new_right: bfloat16 [32, 32, 2048, 128], P('row', 'col')
The draws below stay inside these ranges and needn't reach their ends.
Inputs may be any that keep to these rules, and one draw needn't show every extreme that they name: l_inverse is lower triangular with unit diagonal.
All inputs are finite; a program needn't handle non-finite values.
Results may differ from the reference program's by a relative error of at most 0.0061.
Values may be sent and summed in bfloat16 or wider, within the bound.
No kernel may reach another device: no remote copies, remote signals or barrier semaphores. Data moves between devices by JAX's collectives and lax.ppermute only.
A program may use at most 64 MiB of HBM per device.

```python
import math
import jax
import jax.numpy as jnp
from jax import lax

TILE = 2048
MAX_RANK = 128
PRED_TILES = 32


def draw_l_inverse(key, part):
    below = jax.random.truncated_normal(key, -4.0, 4.0, (TILE, TILE), jnp.float32)
    below = below / math.sqrt(TILE)
    whole = jnp.tril(below, -1) + jnp.eye(TILE, dtype=jnp.float32)
    return whole.astype(jnp.bfloat16)


def plant(values, stream_key, least, top_value):
    shape = values.shape
    index_at = [jax.random.randint(jax.random.fold_in(stream_key, axis), (), 0, shape[axis]) for axis in range(len(shape))]
    values = values.at[tuple(index_at)].set(least)
    longest = shape.index(max(shape))
    index_at[longest] = (index_at[longest] + 1) % shape[longest]
    return values.at[tuple(index_at)].set(top_value)


def block_levels(own_key, shape, pieces, low, largest):
    loudness, own = 1.0, jax.random.fold_in(own_key, 6)
    for axis_at, blocks in pieces:
        steps = jnp.exp(jax.random.uniform(jax.random.fold_in(own, axis_at), (blocks,), jnp.float32, low / len(pieces), largest / len(pieces)))
        loudness = loudness * jnp.repeat(steps, shape[axis_at] // blocks).reshape([-1 if axis == axis_at else 1 for axis in range(len(shape))])
    return loudness


def normal_values(own_key, extent, scale, most, cuts=(), kind=jnp.bfloat16):
    drawn = scale * jax.random.normal(own_key, extent, jnp.float32)
    if cuts:
        drawn = drawn * block_levels(own_key, extent, cuts, -0.22, 0.18)
    return jnp.clip(drawn, -most, most).astype(kind)


def setup_inputs(seed: int = 0) -> dict:
    splits = jax.random.split(jax.random.key(seed), 10)
    return {
        "ba_left": normal_values(splits[0], (PRED_TILES, TILE, MAX_RANK), 1.0, 6.0, ((0, 32), (1, 8))),
        "ba_right": normal_values(splits[1], (PRED_TILES, TILE, MAX_RANK), (MAX_RANK * TILE // 16) ** -0.5, 0.046875, ((0, 32), (1, 8))),
        "l_inverse": draw_l_inverse(jax.random.fold_in(splits[9], 71), 0),
        "aa_left": normal_values(splits[3], (PRED_TILES, PRED_TILES, TILE, MAX_RANK), 1.0, 6.0, ((0, 8), (1, 32))),
        "aa_right": normal_values(splits[4], (PRED_TILES, PRED_TILES, TILE, MAX_RANK), MAX_RANK ** -0.5, 0.5, ((0, 8), (1, 32))),
        "sketch": normal_values(splits[5], (TILE, MAX_RANK), 1.0, 6.0),
        "cross_tile_ranks": plant(jax.random.randint(splits[6], (PRED_TILES,), MAX_RANK // 4, MAX_RANK + 1), jax.random.fold_in(splits[6], 1), MAX_RANK // 4, MAX_RANK).astype(jnp.int32),
        "aa_rank": plant(jax.random.randint(splits[7], (PRED_TILES, PRED_TILES), 3 * MAX_RANK // 4, MAX_RANK + 1), jax.random.fold_in(splits[7], 1), 3 * MAX_RANK // 4, MAX_RANK).astype(jnp.int32),
        "target_rank": plant(jax.random.randint(splits[8], (PRED_TILES, PRED_TILES), MAX_RANK // 8, MAX_RANK // 2 + 1), jax.random.fold_in(splits[8], 1), MAX_RANK // 8, (MAX_RANK // 2 + 1) - 1).astype(jnp.int32),
    }


def refresh(tile_left, tile_right, left_rank, goal_rank, tile_core_matrix, y_rowtile, y_coltile, sketch):
    width = tile_left.shape[0]
    columns = jnp.arange(tile_left.shape[1], dtype=jnp.int32)
    kept_left = tile_left * (columns < left_rank).astype(jnp.bfloat16)
    probes = sketch * (columns < goal_rank).astype(jnp.bfloat16)
    sketch_core = jnp.dot(tile_right.T.astype(jnp.float32), probes.astype(jnp.float32), preferred_element_type=jnp.float32).astype(jnp.bfloat16)
    right_probe = jnp.dot(y_coltile.T.astype(jnp.float32), probes.astype(jnp.float32), preferred_element_type=jnp.float32)
    turned = jnp.dot(tile_core_matrix, right_probe, precision=lax.Precision.HIGHEST).astype(jnp.bfloat16)
    sampled = jnp.dot(kept_left.astype(jnp.float32), sketch_core.astype(jnp.float32), preferred_element_type=jnp.float32) - jnp.dot(y_rowtile.astype(jnp.float32), turned.astype(jnp.float32), preferred_element_type=jnp.float32)
    gram_matrix = jnp.dot(sampled.T, sampled, precision=lax.Precision.HIGHEST) / width
    gram_matrix = gram_matrix + jnp.diag((columns >= goal_rank).astype(jnp.float32))
    lower_cholesky_factor = jnp.linalg.cholesky(gram_matrix)
    inverse_factor = jax.scipy.linalg.solve_triangular(lower_cholesky_factor, jnp.eye(columns.shape[0], dtype=jnp.float32), lower=True)
    new_left = jnp.dot(sampled, inverse_factor.T, precision=lax.Precision.HIGHEST).astype(jnp.bfloat16)
    back_core = jnp.dot(kept_left.T.astype(jnp.float32), new_left.astype(jnp.float32), preferred_element_type=jnp.float32).astype(jnp.bfloat16)
    inner_core = jnp.dot(y_rowtile.T.astype(jnp.float32), new_left.astype(jnp.float32), preferred_element_type=jnp.float32)
    bent = jnp.dot(tile_core_matrix.T, inner_core, precision=lax.Precision.HIGHEST).astype(jnp.bfloat16)
    new_right = (jnp.dot(tile_right.astype(jnp.float32), back_core.astype(jnp.float32), preferred_element_type=jnp.float32) - jnp.dot(y_coltile.astype(jnp.float32), bent.astype(jnp.float32), preferred_element_type=jnp.float32)) / width
    return (new_left, new_right.astype(jnp.bfloat16))

def reference(ba_left, ba_right, l_inverse, aa_left, aa_right, sketch, cross_tile_ranks, aa_rank, target_rank):
    columns = jnp.arange(ba_left.shape[-1], dtype=jnp.int32)
    u_kept = ba_left * (columns[None, None, :] < cross_tile_ranks[:, None, None]).astype(jnp.bfloat16)
    solved = jnp.einsum('ab,jbr->jar', l_inverse.astype(jnp.float32), u_kept.astype(jnp.float32), precision=lax.Precision.HIGHEST).astype(jnp.bfloat16)
    refresh_cols = jax.vmap(refresh, in_axes=(0, 0, 0, 0, 0, None, 0, None))

    def single_tile_row(tile_index):
        x_rowtile = solved[tile_index]
        y_rowtile = ba_right[tile_index]
        tile_core_stack = jnp.einsum('ar,jas->jrs', x_rowtile.astype(jnp.float32), solved.astype(jnp.float32), precision=lax.Precision.HIGHEST)
        return refresh_cols(aa_left[tile_index], aa_right[tile_index], aa_rank[tile_index], target_rank[tile_index], tile_core_stack, y_rowtile, ba_right, sketch)
    lefts, rights = lax.map(single_tile_row, jnp.arange(aa_left.shape[0], dtype=jnp.int32))
    return (lefts, rights)
```

```python
import jax
import jax.numpy as jnp
from jax import lax
from jax.experimental import pallas as pl
from jax.experimental.pallas import tpu as pltpu
from jax.sharding import Mesh
from jax.sharding import PartitionSpec as P

BF = jnp.bfloat16
F32 = jnp.float32
HI = lax.Precision.HIGHEST
TILE = 2048
RANK = 128
GOAL = 64
ROWS = 8
COLS = 32
OWN = 4
ROW = ("x", "yh")
COL = ("yl", "z", "core")
ALL = ("x", "yh", "yl", "z", "core")
SWAP = [(0, 1), (1, 0)]


def to_tile_rows():
    return [
        (r * COLS + c, (c // OWN) * COLS + (c % OWN) * ROWS + r)
        for r in range(ROWS)
        for c in range(COLS)
    ]


def gathered(value, axis, count):
    return lax.all_to_all(
        jnp.broadcast_to(value[None], (count, *value.shape)), axis, 0, 0, tiled=True
    )


def dot_tn(a, b, precision=None):
    return lax.dot_general(
        a, b, (((0,), (0,)), ((), ())), precision=precision, preferred_element_type=F32
    )


def dot_nt(a, b, precision=None):
    return lax.dot_general(
        a, b, (((1,), (1,)), ((), ())), precision=precision, preferred_element_type=F32
    )


def dot_nn(a, b, precision=None):
    return lax.dot_general(
        a, b, (((1,), (0,)), ((), ())), precision=precision, preferred_element_type=F32
    )


def solve_kernel(lt_ref, u_ref, out_ref):
    solved_t = dot_tn(u_ref[...], lt_ref[...]).astype(BF)
    out_ref[...] = dot_nt(lt_ref[...], solved_t).astype(BF)


def solve(l_rows_t, u_whole):
    return pl.pallas_call(
        solve_kernel,
        out_shape=jax.ShapeDtypeStruct((TILE, RANK), BF),
        cost_estimate=pl.CostEstimate(
            flops=4 * TILE * 256 * RANK, bytes_accessed=2 << 20, transcendentals=0
        ),
        name="solve",
    )(l_rows_t, u_whole)


def before_kernel(
    rank_ref, goal_ref, left_ref, right_ref, y_ref, u_ref, sketch_ref,
    gram_ref, probe_ref, turn_ref,
):
    k = pl.program_id(0)
    both = jnp.concatenate([left_ref[0], y_ref[0]], axis=1)
    gram = dot_tn(both, both)
    first = gram.astype(BF)
    rest = gram - first.astype(F32)
    second = rest.astype(BF)
    third = (rest - second.astype(F32)).astype(BF)
    gram_ref[0, 0:256, :] = first
    gram_ref[0, 256:512, :] = second
    gram_ref[0, 512:768, :] = third
    core = dot_tn(right_ref[0], sketch_ref[...])
    row = lax.broadcasted_iota(jnp.int32, (RANK, RANK), 0)
    col = lax.broadcasted_iota(jnp.int32, (RANK, RANK), 1)
    keep = (row < rank_ref[k]) & (col < goal_ref[k])
    probe_ref[0] = jnp.where(keep, core, 0.0).astype(BF)
    turn_ref[0] = u_ref[0].T


def before(ranks, goals, left, right, y_rows, u_rows, sketch):
    tile = pl.BlockSpec((1, TILE, RANK), lambda k, *_: (k, 0, 0))
    return pl.pallas_call(
        before_kernel,
        grid_spec=pltpu.PrefetchScalarGridSpec(
            num_scalar_prefetch=2,
            grid=(OWN,),
            in_specs=[tile, tile, tile, tile, pl.BlockSpec((TILE, RANK), lambda k, *_: (0, 0))],
            out_specs=[
                pl.BlockSpec((1, 768, 256), lambda k, *_: (k, 0, 0)),
                pl.BlockSpec((1, RANK, RANK), lambda k, *_: (k, 0, 0)),
                pl.BlockSpec((1, RANK, TILE), lambda k, *_: (k, 0, 0)),
            ],
        ),
        out_shape=[
            jax.ShapeDtypeStruct((OWN, 768, 256), BF),
            jax.ShapeDtypeStruct((OWN, RANK, RANK), BF),
            jax.ShapeDtypeStruct((OWN, RANK, TILE), BF),
        ],
        cost_estimate=pl.CostEstimate(
            flops=OWN * 2 * TILE * (256 * 256 + RANK * RANK),
            bytes_accessed=12 << 20,
            transcendentals=0,
        ),
        name="before",
    )(ranks, goals, left, right, y_rows, u_rows, sketch)


def whitening(grams):
    lane = lax.broadcasted_iota(jnp.int32, (8, RANK), 1)
    sub = lax.broadcasted_iota(jnp.int32, (8, RANK), 0)
    blocks = []
    for gram in grams:
        own = []
        for b in range(8):
            unit = jnp.where(lane == sub + (8 * b + GOAL), 1.0, 0.0)
            own.append(jnp.where(lane < GOAL, gram[8 * b : 8 * b + 8, :], unit))
        blocks.append(own)
    for k in range(GOAL - 1):
        kb, ks = k // 8, k % 8
        for own in blocks:
            pivot_row = jnp.broadcast_to(own[kb][ks : ks + 1, :], (8, RANK))
            pivot = jnp.broadcast_to(own[kb][ks : ks + 1, k : k + 1], (8, RANK))
            scaled = pivot_row / pivot
            for b in range(kb, 8):
                if b == kb and ks == 7:
                    continue
                column = jnp.broadcast_to(own[b][:, k : k + 1], (8, RANK))
                if b == kb:
                    column = jnp.where(sub > ks, column, 0.0)
                own[b] = own[b] - column * scaled
    factors = []
    for own in blocks:
        done = []
        for b in range(8):
            diagonal = jnp.sum(
                jnp.where(lane == sub + 8 * b, own[b], 0.0), axis=1, keepdims=True
            )
            scale = 1.0 / jnp.sqrt(diagonal)
            moved = pltpu.roll(own[b], GOAL, 1)
            done.append(jnp.where(lane < GOAL, moved * scale, 0.0))
        factors.append(jnp.concatenate(done, axis=0))
    return factors


def after_kernel(
    rank_ref, goal_ref, gram_ref, probe_ref, turn_ref, v_ref, yc_ref, sketch_ref,
    left_hbm, right_hbm, y_hbm,
    out_left, out_right,
    left, right, y_rows, new_left, new_right, in_sem, out_sem,
):
    loads = []
    for n, (source, target) in enumerate(((left_hbm, left), (y_hbm, y_rows), (right_hbm, right))):
        copy = pltpu.make_async_copy(source, target, in_sem.at[n])
        copy.start()
        loads.append(copy)
    row = lax.broadcasted_iota(jnp.int32, (RANK, RANK), 0)
    col = lax.broadcasted_iota(jnp.int32, (RANK, RANK), 1)
    right_probe = dot_tn(yc_ref[...], sketch_ref[...])
    cores, probes, pushed, grams = [], [], [], []
    for k in range(OWN):
        core = dot_nn(turn_ref[k], v_ref[...])
        turned = dot_nn(core, jnp.where(col < goal_ref[k], right_probe, 0.0), HI)
        probe = jnp.concatenate([probe_ref[k], (-turned).astype(BF)], axis=0)
        three = dot_nn(gram_ref[k], probe)
        push = three[0:256] + (three[256:512] + three[512:768])
        gram = dot_tn(probe.astype(F32), push, HI) * (1.0 / TILE)
        gram = gram + jnp.where((row == col) & (col >= goal_ref[k]), 1.0, 0.0)
        cores.append(core)
        probes.append(probe)
        pushed.append(push)
        grams.append(gram[0:GOAL, :])
    factors = whitening(grams)
    zeros = jnp.zeros((RANK - GOAL, RANK), F32)
    for copy in loads:
        copy.wait()
    stores = []
    for k in range(OWN):
        factor = jnp.concatenate([factors[k], zeros], axis=0)
        mixed = dot_nt(probes[k].astype(F32), factor, HI)
        high = mixed.astype(BF)
        low = (mixed - high.astype(F32)).astype(BF)
        both = jnp.concatenate([left[k], y_rows[k]], axis=1)
        new_left[k] = (dot_nn(both, high) + dot_nn(both, low)).astype(BF)
        copy = pltpu.make_async_copy(new_left.at[k], out_left.at[k], out_sem.at[0, k])
        copy.start()
        stores.append(copy)
        seen = dot_nt(pushed[k], factor, HI)
        back = jnp.where(row < rank_ref[k], seen[0:RANK], 0.0).astype(BF)
        bent = dot_tn(cores[k], seen[RANK:], HI).astype(BF)
        pair = jnp.concatenate([right[k], yc_ref[...]], axis=1)
        answer = dot_nn(pair, jnp.concatenate([back, -bent], axis=0))
        new_right[k] = (answer * (1.0 / TILE)).astype(BF)
        copy = pltpu.make_async_copy(new_right.at[k], out_right.at[k], out_sem.at[1, k])
        copy.start()
        stores.append(copy)
    for copy in stores:
        copy.wait()


def after(ranks, goals, gram, probe, turn, v_whole, y_whole, sketch, left, right, y_rows):
    smem = pl.BlockSpec(memory_space=pltpu.SMEM)
    vmem = pl.BlockSpec(memory_space=pltpu.VMEM)
    hbm = pl.BlockSpec(memory_space=pl.ANY)
    whole = jax.ShapeDtypeStruct((OWN, TILE, RANK), BF)
    return pl.pallas_call(
        after_kernel,
        in_specs=[smem, smem] + [vmem] * 6 + [hbm] * 3,
        out_specs=[hbm, hbm],
        out_shape=[whole, whole],
        scratch_shapes=[pltpu.VMEM((OWN, TILE, RANK), BF)] * 5
        + [pltpu.SemaphoreType.DMA((3,)), pltpu.SemaphoreType.DMA((2, OWN))],
        cost_estimate=pl.CostEstimate(
            flops=OWN * 2 * TILE * 256 * RANK * 4, bytes_accessed=16 << 20, transcendentals=0
        ),
        name="after",
    )(ranks, goals, gram, probe, turn, v_whole, y_whole, sketch, left, right, y_rows)


def per_device(
    ba_left, ba_right, l_inverse, aa_left, aa_right, sketch, cross_tile_ranks, aa_rank, target_rank
):
    columns = jnp.arange(RANK, dtype=jnp.int32)
    u_kept = jnp.where(columns[None, :] < cross_tile_ranks[0], ba_left[0], jnp.zeros((), BF))
    ranks, goals = aa_rank[:, 0], target_rank[:, 0]
    left, right = aa_left[:, 0], aa_right[:, 0]
    own = jnp.stack([u_kept, ba_right[0]])
    bulk = lax.all_gather(lax.ppermute(own, ALL, to_tile_rows()), COL, axis=1)
    bulk = bulk.reshape(2, OWN, TILE, RANK)
    u_rows, y_rows = bulk[0], bulk[1]
    l_own = l_inverse.T
    l_pair = lax.ppermute(l_own, "yl", SWAP)
    here = lax.axis_index("yl") == 0
    l_pair = jnp.stack([jnp.where(here, l_own, l_pair), jnp.where(here, l_pair, l_own)])
    l_half = gathered(l_pair, "z", 8)
    l_other = lax.ppermute(l_half, "core", SWAP)
    first = lax.axis_index("core") == 0
    l_rows_t = jnp.stack(
        [jnp.where(first, l_half, l_other), jnp.where(first, l_other, l_half)], axis=2
    )
    l_rows_t = l_rows_t.swapaxes(0, 1).reshape(TILE, 256)
    u_whole = gathered(u_kept, ROW, ROWS).reshape(TILE, RANK)
    y_whole = gathered(ba_right[0], ROW, ROWS).reshape(TILE, RANK)
    v_part = solve(l_rows_t, u_whole)
    v_parts = lax.all_to_all(v_part.reshape(ROWS, 256, RANK), ROW, 0, 0, tiled=True)
    v_own = jnp.sum(v_parts.astype(F32), axis=0).astype(BF)
    v_whole = gathered(v_own, ROW, ROWS).reshape(TILE, RANK)
    gram, probe, turn = before(ranks, goals, left, right, y_rows, u_rows, sketch)
    new_left, new_right = after(
        ranks, goals, gram, probe, turn, v_whole, y_whole, sketch, left, right, y_rows
    )
    return new_left[:, None], new_right[:, None]


def solution(mesh):
    fine = Mesh(mesh.devices.reshape(4, 2, 2, 8, 2), ALL)
    in_specs = (
        P(COL, ROW, None),
        P(COL, ROW, None),
        P(ROW, COL),
        P(ROW, COL, None, None),
        P(ROW, COL, None, None),
        P(),
        P(COL),
        P(ROW, COL),
        P(ROW, COL),
    )
    out_specs = (P(ROW, COL, None, None), P(ROW, COL, None, None))
    return jax.shard_map(
        per_device, mesh=fine, in_specs=in_specs, out_specs=out_specs, check_vma=False
    )
```

```python
import jax
import jax.numpy as jnp
from jax import lax
from jax.experimental import pallas as pl
from jax.experimental.pallas import tpu as pltpu
from jax.sharding import Mesh
from jax.sharding import PartitionSpec as P


BF = jnp.bfloat16
F32 = jnp.float32
TILE = 2048
RANK = 128
GOAL = 64
STEP = 4
ROWS = 8
COLS = 32
OWN = 4
ROW = ("x", "yh")
COL = ("yl", "z", "core")
ALL = ("x", "yh", "yl", "z", "core")
SWAP = [(0, 1), (1, 0)]


ALONG_Z = [
    (z * 2 + core, (z + 1 - 2 * core) % 8 * 2 + core) for z in range(8) for core in range(2)
]


def to_tile_rows():
    pairs = []
    for x in range(4):
        for yh in range(2):
            for tile in range(COLS):
                row, k = divmod(tile, OWN)
                middle = row // 2 % 2 * 4 + row % 2 * 2
                z = (middle + 1 + x if k // 2 else middle - x) % 8
                pairs.append(((x * 2 + yh) * COLS + tile, row * COLS + yh * 16 + z * 2 + k % 2))
    return pairs


def held_rows(yl, z, core):
    middle = lax.rem(lax.axis_index("x"), 2) * 4 + lax.axis_index("yh") * 2
    ahead = lax.rem(z + 8 - middle, 8)
    above = (ahead >= 1) & (ahead <= 4)
    x = jnp.where(above, ahead - 1, lax.rem(8 - ahead, 8))
    return jnp.where(above, 2, 0) + core, pl.multiple_of((x * 2 + yl) * 256, 256)


def place(hop, swapped, other, flipped):
    yl, z, core = lax.axis_index("yl"), lax.axis_index("z"), lax.axis_index("core")
    way = 1 - 2 * core
    return (
        lax.rem(yl + flipped, 2),
        lax.rem(z + 8 + (way if other else -way) * hop, 8),
        lax.rem(core + (1 if other else 0) + swapped, 2),
    )


def dot_tn(a, b, precision=None):
    return lax.dot_general(
        a, b, (((0,), (0,)), ((), ())), precision=precision, preferred_element_type=F32
    )


def dot_nt(a, b, precision=None):
    return lax.dot_general(
        a, b, (((1,), (1,)), ((), ())), precision=precision, preferred_element_type=F32
    )


def dot_nn(a, b, precision=None):
    return lax.dot_general(
        a, b, (((1,), (0,)), ((), ())), precision=precision, preferred_element_type=F32
    )


def keep_kernel(rank_ref, left_ref, right_ref, own_ref, copies_ref):
    col = lax.broadcasted_iota(jnp.int32, (256, RANK), 1)
    kept = jnp.where(col < rank_ref[0], left_ref[0].astype(F32), 0.0).astype(BF)
    own_ref[0] = kept
    own_ref[1] = right_ref[0]
    for n in range(ROWS):
        copies_ref[n, 0] = kept
        copies_ref[n, 1] = right_ref[0]


def keep(rank, left, right):
    vmem = pl.BlockSpec(memory_space=pltpu.VMEM)
    return pl.pallas_call(
        keep_kernel,
        in_specs=[pl.BlockSpec(memory_space=pltpu.SMEM), vmem, vmem],
        out_shape=[
            jax.ShapeDtypeStruct((2, 256, RANK), BF),
            jax.ShapeDtypeStruct((ROWS, 2, 256, RANK), BF),
        ],
        compiler_params=pltpu.CompilerParams(vmem_limit_bytes=60 << 20),
        cost_estimate=pl.CostEstimate(
            flops=256 * RANK, bytes_accessed=1280 << 10, transcendentals=0
        ),
        name="keep",
    )(rank, left, right)


def solve_kernel(*refs):
    pieces, uy_ref, out_ref, lt = refs[:8], refs[8], refs[9], refs[10]
    for n, piece in enumerate(pieces):
        hop, other = (n, False) if n < 5 else (n - 4, True)
        for swapped in range(2):
            for flipped in range(2):
                yl, z, core = place(hop, swapped, other, flipped)
                start = pl.multiple_of((yl * 16 + z * 2 + core) * 64, 64)
                lt[pl.ds(start, 64), :] = piece[swapped, flipped]
    u_whole = uy_ref[:, 0].reshape(TILE, RANK)
    solved_t = dot_tn(u_whole, lt[...]).astype(BF)
    out_ref[...] = dot_nt(lt[...], solved_t).astype(BF).reshape(ROWS, 256, RANK)


def solve(l_pieces, uy):
    return pl.pallas_call(
        solve_kernel,
        out_shape=jax.ShapeDtypeStruct((ROWS, 256, RANK), BF),
        scratch_shapes=[pltpu.VMEM((TILE, 256), BF)],
        compiler_params=pltpu.CompilerParams(vmem_limit_bytes=10 << 20),
        cost_estimate=pl.CostEstimate(
            flops=4 * TILE * 256 * RANK, bytes_accessed=2 << 20, transcendentals=0
        ),
        name="solve",
    )(*l_pieces, uy)


def total_kernel(parts_ref, out_ref):
    total = parts_ref[0].astype(F32)
    for n in range(1, ROWS):
        total = total + parts_ref[n].astype(F32)
    out_ref[...] = total.astype(BF)


def total(parts):
    return pl.pallas_call(
        total_kernel,
        out_shape=jax.ShapeDtypeStruct((256, RANK), BF),
        compiler_params=pltpu.CompilerParams(vmem_limit_bytes=4 << 20),
        cost_estimate=pl.CostEstimate(
            flops=ROWS * 256 * RANK, bytes_accessed=576 << 10, transcendentals=0
        ),
        name="total",
    )(parts)


def probe_kernel(rank_ref, goal_ref, sketch_ref, uy_ref, right_ref, probe_ref, seen_ref):
    k = pl.program_id(0)
    row = lax.broadcasted_iota(jnp.int32, (RANK, RANK), 0)
    col = lax.broadcasted_iota(jnp.int32, (RANK, RANK), 1)
    core = dot_tn(right_ref[0], sketch_ref[...])
    keep = (row < rank_ref[k]) & (col < goal_ref[k])
    probe_ref[0] = jnp.where(keep, core, 0.0).astype(BF)

    @pl.when(k == 0)
    def _():
        seen_ref[...] = dot_tn(uy_ref[:, 1].reshape(TILE, RANK), sketch_ref[...])


def probe(ranks, goals, sketch, uy, right):
    return pl.pallas_call(
        probe_kernel,
        grid_spec=pltpu.PrefetchScalarGridSpec(
            num_scalar_prefetch=2,
            grid=(OWN,),
            in_specs=[
                pl.BlockSpec((TILE, RANK), lambda k, *_: (0, 0)),
                pl.BlockSpec((ROWS, 2, 256, RANK), lambda k, *_: (0, 0, 0, 0)),
                pl.BlockSpec((1, TILE, RANK), lambda k, *_: (k, 0, 0)),
            ],
            out_specs=[
                pl.BlockSpec((1, RANK, RANK), lambda k, *_: (k, 0, 0)),
                pl.BlockSpec((RANK, RANK), lambda k, *_: (0, 0)),
            ],
        ),
        out_shape=[
            jax.ShapeDtypeStruct((OWN, RANK, RANK), BF),
            jax.ShapeDtypeStruct((RANK, RANK), F32),
        ],
        compiler_params=pltpu.CompilerParams(vmem_limit_bytes=10 << 20),
        cost_estimate=pl.CostEstimate(
            flops=(OWN + 1) * 2 * TILE * RANK * RANK, bytes_accessed=4 << 20, transcendentals=0
        ),
        name="probe",
    )(ranks, goals, sketch, uy, right)


def before_kernel(left_hbm, *refs):
    pieces = refs[:16]
    gram_ref, turn_ref, y_ref, left, u_rows, sem, piece_sem = refs[16:]
    load_left = pltpu.make_async_copy(left_hbm, left, sem.at[0])
    load_left.start()
    moves = []
    for n, piece in enumerate(pieces):
        side, hop, other = (n % 2, n // 2, False) if n < 10 else (n % 2, (n - 8) // 2, True)
        for flipped in range(2):
            yl, z, core = place(hop, side, other, flipped)
            tile, start = held_rows(yl, z, core)
            for m, target in enumerate((u_rows, y_ref)):
                moves.append(
                    pltpu.make_async_copy(
                        piece.at[flipped, m],
                        target.at[tile, pl.ds(start, 256), :],
                        piece_sem.at[n, flipped, m],
                    )
                )
    for move in moves:
        move.start()
    for move in moves:
        move.wait()
    load_left.wait()

    @pl.loop(0, OWN)
    def _(k):
        turn_ref[k] = u_rows[k].T
        both = jnp.concatenate([left[k], y_ref[k]], axis=1)
        gram = dot_tn(both, both)
        first = gram.astype(BF)
        rest = gram - first.astype(F32)
        second = rest.astype(BF)
        gram_ref[k, 0:256, :] = first
        gram_ref[k, 256:512, :] = second
        gram_ref[k, 512:768, :] = (rest - second.astype(F32)).astype(BF)


def before(left, pieces):
    vmem = pl.BlockSpec(memory_space=pltpu.VMEM)
    hbm = pl.BlockSpec(memory_space=pl.ANY)
    return pl.pallas_call(
        before_kernel,
        in_specs=[hbm] * 17,
        out_specs=[vmem] * 3,
        out_shape=[
            jax.ShapeDtypeStruct((OWN, 768, 256), BF),
            jax.ShapeDtypeStruct((OWN, RANK, TILE), BF),
            jax.ShapeDtypeStruct((OWN, TILE, RANK), BF),
        ],
        scratch_shapes=[pltpu.VMEM((OWN, TILE, RANK), BF)] * 2
        + [pltpu.SemaphoreType.DMA((1,)), pltpu.SemaphoreType.DMA((16, 2, 2))],
        compiler_params=pltpu.CompilerParams(vmem_limit_bytes=18 << 20),
        cost_estimate=pl.CostEstimate(
            flops=OWN * 2 * TILE * 256 * 256, bytes_accessed=12 << 20, transcendentals=0
        ),
        name="before",
    )(left, *pieces)


def split(a, count):
    pieces = []
    for _ in range(count):
        pieces.append(a.astype(BF))
        a = a - pieces[-1].astype(F32)
    return pieces


def dot_fine(dot, a, b):
    a_high, a_low = split(a, 2)
    b_high, b_low = split(b, 2)
    return dot(a_high, b_high) + (dot(a_high, b_low) + dot(a_low, b_high))


def dot_exact(dot, a, b):
    high, middle, low = split(b, 3)
    return dot(a, high) + (dot(a, middle) + dot(a, low))


def whitening(grams):
    lane = lax.broadcasted_iota(jnp.int32, (8, RANK), 1)
    sub = lax.broadcasted_iota(jnp.int32, (8, RANK), 0)
    blocks = []
    for gram in grams:
        own = []
        for b in range(8):
            unit = jnp.where(lane == sub + (8 * b + GOAL), 1.0, 0.0)
            own.append(jnp.where(lane < GOAL, gram[8 * b : 8 * b + 8, :], unit))
        blocks.append(own)
    for first in range(0, GOAL, STEP):
        kb, top = first // 8, first % 8
        for own in blocks:
            columns = [
                [jnp.broadcast_to(own[b][:, first + j : first + j + 1], (8, RANK)) for j in range(STEP)]
                for b in range(kb, 8)
            ]
            rows = [
                jnp.broadcast_to(own[kb][top + i : top + i + 1, :], (8, RANK)) for i in range(STEP)
            ]
            corner = [
                [
                    jnp.broadcast_to(columns[0][j][top + i : top + i + 1, :], (8, RANK))
                    for j in range(STEP)
                ]
                for i in range(STEP)
            ]
            for j in range(STEP):
                inverse = 1.0 / corner[j][j]
                scaled = rows[j] * inverse
                ratio = [corner[j][m] * inverse for m in range(STEP)]
                for i in range(j + 1, STEP):
                    rows[i] = rows[i] - corner[i][j] * scaled
                    for m in range(j + 1, STEP):
                        corner[i][m] = corner[i][m] - corner[i][j] * ratio[m]
                for b in range(kb, 8):
                    column = columns[b - kb][j]
                    for m in range(j + 1, STEP):
                        columns[b - kb][m] = columns[b - kb][m] - column * ratio[m]
                    if b == kb:
                        column = jnp.where(sub > top + j, column, 0.0)
                    own[b] = own[b] - column * scaled
    factors = []
    for own in blocks:
        done = []
        for b in range(8):
            diagonal = jnp.sum(
                jnp.where(lane == sub + 8 * b, own[b], 0.0), axis=1, keepdims=True
            )
            scale = 1.0 / jnp.sqrt(diagonal)
            moved = pltpu.roll(own[b], GOAL, 1)
            done.append(jnp.where(lane < GOAL, moved * scale, 0.0))
        factors.append(jnp.concatenate(done, axis=0))
    return factors


def after_kernel(
    rank_ref, goal_ref, gram_ref, probe_ref, turn_ref, v0_ref, v1_ref, v2_ref, v3_ref,
    uy_ref, seen_ref, y_rows, left_hbm, right_hbm,
    out_left, out_right,
    left, right, v_ref, new_left, new_right, in_sem, out_sem,
):
    loads = []
    for n, (source, target) in enumerate(((left_hbm, left), (right_hbm, right))):
        copy = pltpu.make_async_copy(source, target, in_sem.at[n])
        copy.start()
        loads.append(copy)
    row = lax.broadcasted_iota(jnp.int32, (RANK, RANK), 0)
    col = lax.broadcasted_iota(jnp.int32, (RANK, RANK), 1)
    x, yh = lax.axis_index("x"), lax.axis_index("yh")
    for n, piece in enumerate((v0_ref, v1_ref, v2_ref, v3_ref)):
        for flipped in range(2):
            block = lax.rem(x + 4 - n, 4) * 2 + lax.rem(yh + flipped, 2)
            v_ref[pl.ds(pl.multiple_of(block * 256, 256), 256), :] = piece[flipped]
    y_whole = uy_ref[:, 1].reshape(TILE, RANK)
    right_probe = seen_ref[...]
    cores, probes, pushed, grams = [], [], [], []
    for k in range(OWN):
        core = dot_nn(turn_ref[k], v_ref[...])
        turned = dot_fine(dot_nn, core, jnp.where(col < goal_ref[k], right_probe, 0.0))
        probe = jnp.concatenate([probe_ref[k], (-turned).astype(BF)], axis=0)
        three = dot_nn(gram_ref[k], probe)
        push = three[0:256] + (three[256:512] + three[512:768])
        gram = dot_exact(dot_tn, probe, push) * (1.0 / TILE)
        gram = gram + jnp.where((row == col) & (col >= goal_ref[k]), 1.0, 0.0)
        cores.append(core)
        probes.append(probe)
        pushed.append(push)
        grams.append(gram[0:GOAL, :])
    factors = whitening(grams)
    zeros = jnp.zeros((RANK - GOAL, RANK), F32)
    mixes, backs, inners = [], [], []
    for k in range(OWN):
        factor = jnp.concatenate([factors[k], zeros], axis=0)
        mixed = dot_exact(dot_nt, probes[k], factor)
        high = mixed.astype(BF)
        mixes.append((high, (mixed - high.astype(F32)).astype(BF)))
        seen = dot_fine(dot_nt, pushed[k], factor)
        backs.append(jnp.where(row < rank_ref[k], seen[0:RANK], 0.0).astype(BF))
        inners.append(seen[RANK:])
    bents = [
        jnp.concatenate([backs[k], -dot_fine(dot_tn, cores[k], inners[k]).astype(BF)], axis=0)
        for k in range(OWN)
    ]
    for copy in loads:
        copy.wait()
    stores = []
    for k in range(OWN):
        high, low = mixes[k]
        both = jnp.concatenate([left[k], y_rows[k]], axis=1)
        new_left[k] = (dot_nn(both, high) + dot_nn(both, low)).astype(BF)
        copy = pltpu.make_async_copy(new_left.at[k], out_left.at[k], out_sem.at[0, k])
        copy.start()
        stores.append(copy)
        pair = jnp.concatenate([right[k], y_whole], axis=1)
        new_right[k] = (dot_nn(pair, bents[k]) * (1.0 / TILE)).astype(BF)
        copy = pltpu.make_async_copy(new_right.at[k], out_right.at[k], out_sem.at[1, k])
        copy.start()
        stores.append(copy)
    for copy in stores:
        copy.wait()


def after(ranks, goals, gram, probes, turn, v_pieces, uy, seen, y_rows, left, right):
    smem = pl.BlockSpec(memory_space=pltpu.SMEM)
    vmem = pl.BlockSpec(memory_space=pltpu.VMEM)
    hbm = pl.BlockSpec(memory_space=pl.ANY)
    whole = jax.ShapeDtypeStruct((OWN, TILE, RANK), BF)
    tiles = pltpu.VMEM((OWN, TILE, RANK), BF)
    return pl.pallas_call(
        after_kernel,
        in_specs=[smem, smem] + [vmem] * 10 + [hbm] * 2,
        out_specs=[hbm, hbm],
        out_shape=[whole, whole],
        scratch_shapes=[tiles, tiles, pltpu.VMEM((TILE, RANK), BF), tiles, tiles]
        + [pltpu.SemaphoreType.DMA((2,)), pltpu.SemaphoreType.DMA((2, OWN))],
        compiler_params=pltpu.CompilerParams(vmem_limit_bytes=24 << 20),
        cost_estimate=pl.CostEstimate(
            flops=OWN * 2 * TILE * 256 * RANK * 4, bytes_accessed=16 << 20, transcendentals=0
        ),
        name="after",
    )(ranks, goals, gram, probes, turn, *v_pieces, uy, seen, y_rows, left, right)


def swap(value, axis):
    return lax.ppermute(value, axis, SWAP)


def ring(value):
    return lax.ppermute(value, ("z", "core"), ALONG_Z)


def exchange(value):
    return lax.all_to_all(value, ROW, 0, 0, tiled=True)


def on_device(
    ba_left, ba_right, l_inverse, aa_left, aa_right, sketch, cross_tile_ranks, aa_rank, target_rank
):
    ranks, goals = aa_rank[:, 0], target_rank[:, 0]
    left, right = aa_left[:, 0], aa_right[:, 0]
    own, copies = keep(cross_tile_ranks, ba_left, ba_right)

    l_own = l_inverse.T
    l_pair = jnp.stack([l_own, swap(l_own, "yl")])
    l_chips = jnp.stack([l_pair, swap(l_pair, "core")])
    l_mine = [l_chips]
    for _ in range(1, 5):
        l_mine.append(ring(l_mine[-1]))
    l_pieces = l_mine + [swap(l_mine[hop], "core") for hop in range(1, 4)]
    uy = exchange(copies)

    moved = lax.ppermute(own, ALL, to_tile_rows())
    near = jnp.stack([moved, swap(moved, "yl")])
    mine = [(near, swap(near, "core"))]
    for _ in range(1, 5):
        mine.append((ring(mine[-1][0]), ring(mine[-1][1])))
    pieces = [half for pair in mine for half in pair]
    for hop in range(1, 4):
        pieces += [swap(mine[hop][0], "core"), swap(mine[hop][1], "core")]
    probes, seen = probe(ranks, goals, sketch, uy, right)
    gram, turn, y_rows = before(left, pieces)

    v_own = total(exchange(solve(l_pieces, uy)))
    v_pieces = [jnp.stack([v_own, swap(v_own, "yh")])]
    for hop in range(1, 4):
        v_pieces.append(
            lax.ppermute(v_pieces[0], "x", [(x, (x + hop) % 4) for x in range(4)])
        )
    new_left, new_right = after(
        ranks, goals, gram, probes, turn, v_pieces, uy, seen, y_rows, left, right
    )
    return new_left[:, None], new_right[:, None]


def solution(mesh):
    fine = Mesh(mesh.devices.reshape(4, 2, 2, 8, 2), ALL)
    in_specs = (
        P(COL, ROW, None),
        P(COL, ROW, None),
        P(ROW, COL),
        P(ROW, COL, None, None),
        P(ROW, COL, None, None),
        P(),
        P(COL),
        P(ROW, COL),
        P(ROW, COL),
    )
    out_specs = (P(ROW, COL, None, None), P(ROW, COL, None, None))
    return jax.shard_map(
        on_device, mesh=fine, in_specs=in_specs, out_specs=out_specs, check_vma=False
    )
```
